32 devices in a mesh: gz: 4 (over y, core), xy: 8 (over z, x).
Axes of the slice: x: 2, y: 2, z: 4, core: 2. Of those that a mesh axis runs over, the one named last changes fastest.
Arguments:
- volume: bfloat16 [32, 64, 2048], P('gz', 'xy'), may hold values from -6 to 6
- backbone_weight: bfloat16 [64, 1728], replicated, may hold values from -0.15625 to 0.15625
- refine_weight: bfloat16 [64, 1728], replicated, may hold values from -0.15625 to 0.15625
- mix_weight: bfloat16 [64, 64], replicated, may hold values from -0.75 to 0.75
- tile_cot: bfloat16 [4, 8, 8, 2, 8, 8, 512], P('gz', 'xy'), may hold values from -6 to 6
- tile_slot: int32 [4, 8, 8, 2], P('gz', 'xy'), may hold values from 0 to 3
- tile_count: int32 [4, 8, 8], P('gz'), may hold values from 0 to 2, as said below
Outputs:
- volume_grad: bfloat16 [32, 64, 2048], P('gz', 'xy')
- backbone_step: float32 [64, 1728], replicated
- refine_step: float32 [64, 1728], replicated
- mix_step: float32 [64, 64], replicated
The draws below stay inside these ranges and needn't reach their ends.
Inputs may be any that keep to these rules, and one draw needn't show every extreme that they name: `tile_count`: in every slab each owner receives exactly 8 live slots in all; some pairs of brick and owner use all 2 slots. `tile_slot`: only slots j < tile_count[g, s, d] are read.
All inputs are finite; a program needn't handle non-finite values.
Results may differ from the reference program's by a relative error of at most 0.0059.
Values may be sent and summed in bfloat16 or wider, within the bound.
A program may use at most 192 MiB of HBM per device.

```python
import jax
import jax.numpy as jnp
from jax import lax

C = 64
TE = 8
CAP = 2
BZ = 8
BY = 8
NX = 32
NZ = 32
NY = 64
TPB = 4
OWN = 8
N_GZ = 4
N_XY = 8


def draw_tile_count(key, part):
    heavy_count = N_XY // 8
    light_count = N_XY - heavy_count

    def one_slab(slab_key):
        order_key, shift_key = jax.random.split(slab_key)
        source_rank = jax.random.permutation(order_key, N_XY).astype(jnp.int32)
        shifts = jax.random.randint(shift_key, (N_XY,), 0, light_count).astype(jnp.int32)
        light_rank = jnp.clip(source_rank - heavy_count, 0, light_count - 1)
        pattern = jnp.where((light_rank[:, None] + shifts[None, :]) % light_count % 3 == 0, CAP, 0)
        return jnp.where(source_rank[:, None] < heavy_count, CAP, pattern).astype(jnp.int32)
    return jax.vmap(one_slab)(jax.random.split(key, N_GZ))


def plant(values, key, smallest, high):
    longest = values.shape.index(max(values.shape))
    spots = []
    for shift in (0, 1):
        where = [jax.random.randint(jax.random.fold_in(key, axis), (), 0, length) for axis, length in enumerate(values.shape)]
        where[longest] = (where[longest] + shift) % values.shape[longest]
        spots.append(tuple(where))
    return values.at[spots[0]].set(smallest).at[spots[1]].set(high)


def steps_of(key, shape, pieces, low, top_value):
    def one(dim, shards_of):
        heights = jax.random.uniform(jax.random.fold_in(jax.random.fold_in(key, 6), dim), (shards_of,), jnp.float32, low / len(pieces), top_value / len(pieces))
        return jnp.repeat(jnp.exp(heights), shape[dim] // shards_of).reshape((-1,) + (1,) * (len(shape) - dim - 1))

    factor_of = one(*pieces[0])
    for cut in pieces[1:]:
        factor_of = factor_of * one(*cut)
    return factor_of


def centred(own_key, dims, scale, most, shards=(), held_as=jnp.bfloat16):
    factor_of = steps_of(own_key, dims, shards, -0.22, 0.18) if shards else 1.0
    array = jax.random.normal(own_key, dims, jnp.float32) * scale * factor_of
    return jnp.minimum(jnp.maximum(array, -most), most).astype(held_as)


def setup_inputs(seed: int = 0) -> dict:
    arg_keys = jax.random.split(jax.random.key(seed), 8)
    return {
        "volume": centred(arg_keys[0], (NZ, NY, NX * C), 1.0, 6.0, ((0, 4), (1, 8))),
        "backbone_weight": centred(arg_keys[1], (C, 27 * C), (27 * C) ** -0.5, 0.15625),
        "refine_weight": centred(arg_keys[2], (C, 27 * C), (27 * C) ** -0.5, 0.15625),
        "mix_weight": centred(arg_keys[3], (C, C), C ** -0.5, 0.75),
        "tile_cot": centred(arg_keys[4], (N_GZ, N_XY, N_XY, CAP, TE, TE, TE * C), 1.0, 6.0, ((0, 4), (1, 8))),
        "tile_slot": plant(jax.random.randint(arg_keys[5], (N_GZ, N_XY, N_XY, CAP), 0, TPB), jax.random.fold_in(arg_keys[5], 1), 0, TPB - 1).astype(jnp.int32),
        "tile_count": draw_tile_count(jax.random.fold_in(arg_keys[7], 71), 0),
    }


EPSILON = 1e-06

def offset_list():
    return [(step_z, step_y, step_x) for step_z in range(3) for step_y in range(3) for step_x in range(3)]

def narrowed(values):
    return lax.optimization_barrier(values.astype(jnp.bfloat16)).astype(jnp.float32)

def pad_cells(values):
    widths = [(0, 0)] * (values.ndim - 4) + [(1, 1), (1, 1), (1, 1), (0, 0)]
    return jnp.pad(values, widths)

def window_at(padded, corner, extent):
    return padded[..., corner[0]:corner[0] + extent[0], corner[1]:corner[1] + extent[1], corner[2]:corner[2] + extent[2], :]

def conv_apply(padded, weight, extent):
    channels = padded.shape[-1]
    result = None
    for offset_id, corner in enumerate(offset_list()):
        kernel = weight[:, offset_id * channels:(offset_id + 1) * channels]
        summand = jnp.einsum('...i,io->...o', window_at(padded, corner, extent), kernel)
        result = summand if result is None else result + summand
    return result

def conv_transpose(padded_grad, weight, extent):
    channels = padded_grad.shape[-1]
    result = None
    for offset_id, corner in enumerate(offset_list()):
        kernel = weight[:, offset_id * channels:(offset_id + 1) * channels]
        mirror = (2 - corner[0], 2 - corner[1], 2 - corner[2])
        summand = jnp.einsum('...o,io->...i', window_at(padded_grad, mirror, extent), kernel)
        result = summand if result is None else result + summand
    return result

def conv_weight_grad(padded, grad, extent):
    channels = padded.shape[-1]
    flat_grad = grad.reshape(-1, channels)
    blocks = []
    for corner in offset_list():
        window = window_at(padded, corner, extent).reshape(-1, channels)
        blocks.append(jnp.dot(window.T, flat_grad, precision=lax.Precision.HIGHEST))
    return jnp.concatenate(blocks, axis=1)

def normalized(gradient):
    return gradient / jnp.sqrt(jnp.mean(gradient * gradient) + EPSILON)

def refine_tiles(tiles, cots, refine_weight, mix_weight):
    batch_size = tiles.shape[0]
    tile_edge = tiles.shape[1]
    channels = mix_weight.shape[0]
    extent = (tile_edge, tile_edge, tile_edge)
    shaped = tiles.reshape(batch_size, tile_edge, tile_edge, tile_edge, channels).astype(jnp.float32)
    upstream = cots.reshape(batch_size, tile_edge, tile_edge, tile_edge, channels).astype(jnp.float32)
    weight_one = refine_weight.astype(jnp.float32)
    weight_two = mix_weight.astype(jnp.float32)
    padded = pad_cells(shaped)
    before = conv_apply(padded, weight_one, extent)
    gated_act = narrowed(jax.nn.silu(before))
    mix_part = jnp.dot(gated_act.reshape(-1, channels).T, upstream.reshape(-1, channels), precision=lax.Precision.HIGHEST)
    gated_grad = jnp.einsum('...o,io->...i', upstream, weight_two)
    sigmoid_of = jax.nn.sigmoid(before)
    before_grad = narrowed(gated_grad * sigmoid_of * (1.0 + before * (1.0 - sigmoid_of)))
    refine_part = conv_weight_grad(padded, before_grad, extent)
    tile_grad = upstream + conv_transpose(pad_cells(before_grad), weight_one, extent)
    return (tile_grad.astype(jnp.bfloat16).reshape(tiles.shape), refine_part, mix_part)

def reference(volume, backbone_weight, refine_weight, mix_weight, tile_cot, tile_slot, tile_count):
    field = volume.astype(jnp.float32).reshape(NZ, NY, NX, C)
    padded_in = pad_cells(field)
    weight_back = backbone_weight.astype(jnp.float32)
    feature = (field + conv_apply(padded_in, weight_back, (NZ, NY, NX))).astype(jnp.bfloat16)
    blocked = feature.reshape(N_GZ, BZ // TE, TE, N_XY, BY // TE, TE, NX // TE, TE, C)
    all_tiles = blocked.transpose(0, 3, 1, 4, 6, 2, 5, 7, 8).reshape(N_GZ, N_XY * TPB, TE, TE, TE * C)
    slot_total = N_XY * CAP
    lanes_cap = jnp.arange(CAP, dtype=jnp.int32)

    def per_owner(pair_id):
        slab_id = pair_id // N_XY
        owner_id = pair_id % N_XY
        counts_in = jnp.take(tile_count[slab_id], owner_id, axis=1)
        slots_in = jnp.take(tile_slot[slab_id], owner_id, axis=1)
        cots_in = jnp.take(tile_cot[slab_id], owner_id, axis=1).reshape(slot_total, TE, TE, TE * C)
        valid_slot = (lanes_cap[None, :] < counts_in[:, None]).reshape(slot_total)
        slot_rank = jnp.cumsum(valid_slot.astype(jnp.int32)) - 1
        chooser = (slot_rank[None, :] == jnp.arange(OWN, dtype=jnp.int32)[:, None]) & valid_slot[None, :]
        source_rows = (jnp.arange(N_XY, dtype=jnp.int32)[:, None] * TPB + slots_in).reshape(slot_total)
        tile_rows = lax.optimization_barrier(jnp.sum(jnp.where(chooser, source_rows[None, :], 0), axis=1)).astype(jnp.int32)
        slot_rows = lax.optimization_barrier(jnp.sum(jnp.where(chooser, jnp.arange(slot_total, dtype=jnp.int32)[None, :], 0), axis=1)).astype(jnp.int32)
        chosen = jnp.take(all_tiles[slab_id], tile_rows, axis=0)
        chosen_cot = jnp.take(cots_in, slot_rows, axis=0)
        tile_grad, refine_part, mix_part = refine_tiles(chosen, chosen_cot, refine_weight, mix_weight)
        return (tile_grad, refine_part, mix_part, (slab_id * (N_XY * TPB) + tile_rows).astype(jnp.int32))
    tile_grads, refine_parts, mix_parts, segment_ids = lax.map(per_owner, jnp.arange(N_GZ * N_XY, dtype=jnp.int32))
    summed = jax.ops.segment_sum(tile_grads.astype(jnp.float32).reshape(N_GZ * N_XY * OWN, TE * TE * TE * C), segment_ids.reshape(-1), num_segments=N_GZ * N_XY * TPB)
    placed = summed.reshape(N_GZ, N_XY, BZ // TE, BY // TE, NX // TE, TE, TE, TE, C).transpose(0, 2, 5, 1, 3, 6, 4, 7, 8)
    feature_grad = narrowed(placed.reshape(NZ, NY, NX, C))
    volume_grad = (feature_grad + conv_transpose(pad_cells(feature_grad), weight_back, (NZ, NY, NX))).astype(jnp.bfloat16).reshape(NZ, NY, NX * C)
    backbone_sum = conv_weight_grad(padded_in, feature_grad, (NZ, NY, NX))
    return (volume_grad, normalized(backbone_sum), normalized(lax.optimization_barrier(jnp.sum(refine_parts, axis=0))), normalized(lax.optimization_barrier(jnp.sum(mix_parts, axis=0))))
```

```python
import functools

import jax
import jax.numpy as jnp
from jax import lax
from jax.experimental import pallas as pl
from jax.experimental.pallas import tpu as pltpu
from jax.sharding import PartitionSpec as P

EPSILON = 1e-06
F32 = jnp.float32
BF16 = jnp.bfloat16
VMEM = pl.BlockSpec(memory_space=pltpu.VMEM)


def with_rims(block, sides):
    for axis, dim in sides:
        count = lax.axis_size(axis)
        forward = [(i, i + 1) for i in range(count - 1)]
        backward = [(target, source) for source, target in forward]
        size = block.shape[dim]
        low = lax.ppermute(lax.slice_in_dim(block, size - 1, None, axis=dim), axis, forward)
        high = lax.ppermute(lax.slice_in_dim(block, 0, 1, axis=dim), axis, backward)
        block = jnp.concatenate([low, block, high], axis=dim)
    return block


def banded(blocks):
    w0, w1, w2 = blocks[:, 0], blocks[:, 1], blocks[:, 2]
    zero = jnp.zeros_like(w0)
    left = jnp.concatenate([w1, w2, zero, w0], axis=1)
    right = jnp.concatenate([w0, w1, w2, zero], axis=1)
    both = jnp.concatenate([left, right], axis=2)
    return both.reshape(-1, both.shape[2])


def forward_band(weight, channels):
    return banded(weight.reshape(channels, 9, 3, channels).transpose(1, 2, 0, 3))


def backward_band(weight, channels):
    blocks = weight.reshape(channels, 9, 3, channels).transpose(1, 2, 3, 0)
    return banded(blocks[::-1, ::-1])


def side_lanes(cells, half, period):
    pairs = cells.shape[1]
    lane = lax.broadcasted_iota(jnp.int32, cells.shape, 2)
    place = lax.broadcasted_iota(jnp.int32, cells.shape, 1) % period
    right = pltpu.roll(cells, pairs - 1, 1)
    left = pltpu.roll(cells, 1, 1)
    low = lane < half
    right = jnp.where(place == period - 1, 0.0, right)
    left = jnp.where(place == 0, 0.0, left)
    return jnp.where(low, right, left)


def fill_windows(target, source, half, period, inner):
    depth = target.shape[0]
    lanes = 2 * half
    if inner:
        target[...] = jnp.zeros_like(target)
    first, last = (1, depth - 1) if inner else (0, depth)
    for z in range(first, last):
        cells = source(z - first)
        rows = pl.ds(1, target.shape[1] - 2) if inner else pl.ds(0, target.shape[1])
        target[z, rows, :, pl.ds(0, lanes)] = cells.astype(BF16)
        target[z, rows, :, pl.ds(lanes, lanes)] = side_lanes(cells.astype(F32), half, period).astype(
            BF16
        )


def window_rows(windows, z, count, dz, dy):
    rows = windows.shape[1] - 2
    pairs, width = windows.shape[2], windows.shape[3]
    part = windows[pl.ds(z + dz, count), pl.ds(dy, rows)]
    return part.reshape(count * rows * pairs, width)


def conv_rows(windows, weight, z, count):
    parts = [window_rows(windows, z, count, dz, dy) for dz in range(3) for dy in range(3)]
    return jnp.dot(jnp.concatenate(parts, axis=1), weight[...], preferred_element_type=F32)


def outer_sums(out, base, windows, grad_turned, half):
    depth = windows.shape[0] - 2
    lanes = 2 * half
    lane = lax.broadcasted_iota(jnp.int32, (half, lanes), 1)
    held = None
    for offset in range(9):
        both = jnp.dot(
            grad_turned,
            window_rows(windows, 0, depth, offset // 3, offset % 3),
            preferred_element_type=F32,
        )
        top_near, top_far = both[:half, :lanes], both[:half, lanes:]
        far_turned = pltpu.roll(top_far, half, 1)
        near_turned = pltpu.roll(top_near, half, 1)
        first = jnp.where(lane < half, far_turned, near_turned) + both[half:, :lanes]
        third = near_turned + both[half:, lanes:]
        out[pl.ds(base + offset * half, half), :] = first.astype(BF16)
        if offset % 2 == 0:
            held = jnp.where(lane < half, third, 0.0)
        else:
            pair = held + jnp.where(lane < half, 0.0, pltpu.roll(third, half, 1))
            out[pl.ds(base + (9 + offset // 2) * half, half), :] = pair.astype(BF16)
    out[pl.ds(base + 13 * half, half), :] = held.astype(BF16)


def refine_kernel(
    period, vol, cot, wb, wr, wrt, mix2, fgrad, rsum, msum, xw, fw, pw, pre_s, gate_s, pg_s
):
    depth, rows, pairs, lanes = fgrad.shape
    half = lanes // 2
    step = 4 if depth % 4 == 0 else depth
    flat = step * rows * pairs
    fill_windows(xw, lambda z: vol[z], half, pairs, False)
    fw[...] = jnp.zeros_like(fw)
    pw[...] = jnp.zeros_like(pw)
    inner = pl.ds(1, rows)

    def put(target, z, cells):
        target[pl.ds(z + 1, step), inner, :, pl.ds(0, lanes)] = cells.astype(BF16)
        near = cells.astype(F32).reshape(step * rows, pairs, lanes)
        target[pl.ds(z + 1, step), inner, :, pl.ds(lanes, lanes)] = (
            side_lanes(near, half, period).astype(BF16).reshape(step, rows, pairs, lanes)
        )

    for z in range(0, depth, step):
        own = vol[pl.ds(z + 1, step), inner].astype(F32).reshape(flat, lanes)
        feature = (own + conv_rows(xw, wb, z, step)).astype(BF16)
        put(fw, z, feature.reshape(step, rows, pairs, lanes))
    for z in range(0, depth, step):
        pre = conv_rows(fw, wr, z, step)
        sig = jax.nn.sigmoid(pre)
        total = cot[pl.ds(z, step)].reshape(flat, lanes).astype(BF16)
        gate_s[pl.ds(z * rows * pairs, flat), :] = (pre * sig).astype(BF16)
        gated_grad = jnp.dot(total, mix2[...], preferred_element_type=F32)
        pre_grad = (gated_grad * sig * (1.0 + pre * (1.0 - sig))).astype(BF16)
        pg_s[pl.ds(z * rows * pairs, flat), :] = pre_grad
        put(pw, z, pre_grad.reshape(step, rows, pairs, lanes))
    for z in range(0, depth, step):
        total = cot[pl.ds(z, step)].reshape(flat, lanes)
        grad = total + conv_rows(pw, wrt, z, step)
        fgrad[pl.ds(z, step)] = grad.astype(BF16).reshape(step, rows, pairs, lanes)
    outer_sums(rsum, 0, fw, pg_s[...].T, half)
    cot_rows = cot[...].reshape(depth * rows * pairs, lanes).astype(BF16)
    both = jnp.dot(gate_s[...].T, cot_rows, preferred_element_type=F32)
    lane = lax.broadcasted_iota(jnp.int32, (half, lanes), 1)
    msum[...] = jnp.where(lane < half, both[:half] + pltpu.roll(both[half:], half, 1), 0.0).astype(
        BF16
    )


def backbone_kernel(vol, grad, wbt, rsum, msum, vgrad, sums, xw, gw):
    depth, rows, pairs, lanes = vgrad.shape
    half = lanes // 2
    step = 4 if depth % 4 == 0 else depth
    flat = step * rows * pairs
    fill_windows(xw, lambda z: vol[z], half, pairs, False)
    fill_windows(gw, lambda z: grad[z], half, pairs, False)
    inner = pl.ds(1, rows)
    for z in range(0, depth, step):
        own = grad[pl.ds(z + 1, step), inner].astype(F32).reshape(flat, lanes)
        out = own + conv_rows(gw, wbt, z, step)
        vgrad[pl.ds(z, step)] = out.astype(BF16).reshape(step, rows, pairs, lanes)
    own = grad[pl.ds(1, depth), inner].reshape(depth * rows * pairs, lanes)
    outer_sums(sums, 0, xw, own.T, half)
    block = rsum.shape[0]
    sums[pl.ds(block, block), :] = rsum[...]
    sums[pl.ds(2 * block, half), :] = msum[...]
    used = 2 * block + half
    if used < sums.shape[0]:
        sums[pl.ds(used, sums.shape[0] - used), :] = jnp.zeros(
            (sums.shape[0] - used, lanes), BF16
        )


def total_kernel(
    sizes, counts, n_xy, total_devices, sums, out, got, mine, gathered, send1, recv1, send2, recv2
):
    me = lax.axis_index("gz") * n_xy + lax.axis_index("xy")
    chunk = mine.shape[0]
    barrier = pltpu.get_barrier_semaphore()

    def peer(step):
        target = lax.rem(me + step, total_devices)
        return target, (lax.div(target, n_xy), lax.rem(target, n_xy))

    def greet(step, carry):
        _, where = peer(step)
        pl.semaphore_signal(barrier, inc=1, device_id=where, device_id_type=pl.DeviceIdType.MESH)
        return carry

    lax.fori_loop(1, total_devices, greet, 0)
    pl.semaphore_wait(barrier, total_devices - 1)

    def scatter(step):
        target, where = peer(step)
        return pltpu.make_async_remote_copy(
            src_ref=sums.at[pl.ds(target * chunk, chunk)],
            dst_ref=got.at[step],
            send_sem=send1.at[step],
            recv_sem=recv1.at[step],
            device_id=where,
            device_id_type=pl.DeviceIdType.MESH,
        )

    def gather(step):
        _, where = peer(step)
        return pltpu.make_async_remote_copy(
            src_ref=mine,
            dst_ref=gathered.at[step],
            send_sem=send2.at[step],
            recv_sem=recv2.at[step],
            device_id=where,
            device_id_type=pl.DeviceIdType.MESH,
        )

    def start1(step, carry):
        scatter(step).start()
        return carry

    lax.fori_loop(1, total_devices, start1, 0)

    def add(step, total):
        scatter(step).wait_recv()
        return total + got[step].astype(F32)

    own = sums[pl.ds(me * chunk, chunk), :].astype(F32)
    mine[...] = lax.fori_loop(1, total_devices, add, own).astype(BF16)

    def start2(step, carry):
        gather(step).start()
        return carry

    lax.fori_loop(1, total_devices, start2, 0)

    def end1(step, carry):
        scatter(step).wait_send()
        return carry

    lax.fori_loop(1, total_devices, end1, 0)
    out[pl.ds(me * chunk, chunk), :] = mine[...].astype(F32)

    def place(step, carry):
        gather(step).wait_recv()
        source = lax.rem(me + total_devices - step, total_devices)
        out[pl.ds(source * chunk, chunk), :] = gathered[step].astype(F32)
        return carry

    lax.fori_loop(1, total_devices, place, 0)

    def end2(step, carry):
        gather(step).wait_send()
        return carry

    lax.fori_loop(1, total_devices, end2, 0)
    base = 0
    for size, count in zip(sizes, counts):
        values = out[pl.ds(base, size), :]
        mean = jnp.sum(jnp.sum(values * values, axis=0, keepdims=True), axis=1, keepdims=True) / count
        out[pl.ds(base, size), :] = values / jnp.sqrt(mean + EPSILON)
        base += size


def unpacked(values, channels):
    near = values[: 9 * channels].reshape(9, channels, 2, channels).transpose(3, 0, 2, 1)
    far = values[9 * channels :].reshape(5, channels, 2, channels).transpose(3, 0, 2, 1)
    far = far.reshape(channels, 10, 1, channels)[:, :9]
    return jnp.concatenate([near, far], axis=2).reshape(channels, 27 * channels)


def body(volume, backbone_weight, refine_weight, mix_weight, tile_cot, tile_slot, tile_count):
    depth, rows, width = volume.shape
    channels = mix_weight.shape[0]
    edge = tile_cot.shape[4]
    owners, capacity = tile_cot.shape[2], tile_cot.shape[3]
    assert depth == edge and rows == edge
    lanes = 2 * channels
    pairs = width // lanes
    period = edge // 2
    tiles = pairs // period
    slots = owners * capacity
    n_gz, n_xy = lax.axis_size("gz"), lax.axis_size("xy")
    devices = n_gz * n_xy
    brick = (depth, rows, pairs, lanes)
    rimmed = with_rims(volume, (("gz", 0), ("xy", 1)))
    rimmed = rimmed.reshape(depth + 2, rows + 2, pairs, lanes)

    my_counts = jnp.sum(
        tile_count[0]
        * (jnp.arange(owners, dtype=jnp.int32) == lax.axis_index("xy")).astype(jnp.int32)[:, None],
        axis=0,
    )
    live = (jnp.arange(capacity, dtype=jnp.int32)[None, :] < my_counts[:, None]).reshape(slots)
    picker = (
        (tile_slot.reshape(slots)[None, :] == jnp.arange(tiles, dtype=jnp.int32)[:, None])
        & live[None, :]
    ).astype(BF16)
    cot = jnp.dot(
        picker, tile_cot.reshape(slots, edge * edge * edge * channels), preferred_element_type=F32
    )
    cot = cot.reshape(tiles, depth, rows, period, lanes).transpose(1, 2, 0, 3, 4).reshape(brick)

    mix_turned = mix_weight.T
    blank = jnp.zeros_like(mix_turned)
    mix2 = jnp.concatenate(
        [
            jnp.concatenate([mix_turned, blank], axis=1),
            jnp.concatenate([blank, mix_turned], axis=1),
        ],
        axis=0,
    )
    block = 14 * channels
    framed = (depth + 2, rows + 2, pairs, 2 * lanes)
    params = pltpu.CompilerParams(vmem_limit_bytes=56 * 1024 * 1024)
    fgrad, rsum, msum = pl.pallas_call(
        functools.partial(refine_kernel, period),
        out_shape=(
            jax.ShapeDtypeStruct(brick, BF16),
            jax.ShapeDtypeStruct((block, lanes), BF16),
            jax.ShapeDtypeStruct((channels, lanes), BF16),
        ),
        in_specs=[VMEM] * 6,
        out_specs=(VMEM,) * 3,
        scratch_shapes=[
            pltpu.VMEM(framed, BF16),
            pltpu.VMEM(framed, BF16),
            pltpu.VMEM(framed, BF16),
            pltpu.VMEM((8, lanes), F32),
            pltpu.VMEM((depth * rows * pairs, lanes), BF16),
            pltpu.VMEM((depth * rows * pairs, lanes), BF16),
        ],
        compiler_params=params,
    )(
        rimmed,
        cot,
        forward_band(backbone_weight, channels),
        forward_band(refine_weight, channels),
        backward_band(refine_weight, channels),
        mix2,
    )
    grad_rimmed = with_rims(fgrad, (("gz", 0), ("xy", 1)))
    used = 2 * block + channels
    chunk = -(-used // (devices * 16)) * 16
    vgrad, sums = pl.pallas_call(
        backbone_kernel,
        out_shape=(
            jax.ShapeDtypeStruct(brick, BF16),
            jax.ShapeDtypeStruct((devices * chunk, lanes), BF16),
        ),
        in_specs=[VMEM] * 5,
        out_specs=(VMEM,) * 2,
        scratch_shapes=[pltpu.VMEM(framed, BF16), pltpu.VMEM(framed, BF16)],
        compiler_params=params,
    )(rimmed, grad_rimmed, backward_band(backbone_weight, channels), rsum, msum)
    sizes = (block, block, channels)
    counts = (27.0 * channels * channels, 27.0 * channels * channels, 1.0 * channels * channels)
    totals = pl.pallas_call(
        functools.partial(total_kernel, sizes, counts, n_xy, devices),
        out_shape=jax.ShapeDtypeStruct((devices * chunk, lanes), F32),
        in_specs=[VMEM],
        out_specs=VMEM,
        scratch_shapes=[
            pltpu.VMEM((devices, chunk, lanes), BF16),
            pltpu.VMEM((chunk, lanes), BF16),
            pltpu.VMEM((devices, chunk, lanes), BF16),
        ]
        + [pltpu.SemaphoreType.DMA((devices,))] * 4,
        compiler_params=pltpu.CompilerParams(collective_id=0, has_side_effects=True),
    )(sums)
    return (
        vgrad.reshape(depth, rows, width),
        unpacked(totals[:block], channels),
        unpacked(totals[block : 2 * block], channels),
        totals[2 * block : used, :channels],
    )


def solution(mesh):
    in_specs = (
        P("gz", "xy", None),
        P(),
        P(),
        P(),
        P("gz", "xy", None, None, None, None, None),
        P("gz", "xy", None, None),
        P("gz", None, None),
    )
    out_specs = (P("gz", "xy", None), P(), P(), P())
    return jax.shard_map(body, mesh=mesh, in_specs=in_specs, out_specs=out_specs, check_vma=False)
```

```python
import functools

import jax
import jax.numpy as jnp
from jax import lax
from jax.experimental import pallas as pl
from jax.experimental.pallas import tpu as pltpu
from jax.sharding import PartitionSpec as P

EPSILON = 1e-06
F32 = jnp.float32
BF16 = jnp.bfloat16
VMEM = pl.BlockSpec(memory_space=pltpu.VMEM)


def neighbours():
    return [(dz, dy) for dz in (-1, 0, 1) for dy in (-1, 0, 1) if (dz, dy) != (0, 0)]


def rim_kernel(n_gz, n_xy, block, framed, send, recv):
    depth, rows = block.shape[0], block.shape[1]
    gz, xy = lax.axis_index("gz"), lax.axis_index("xy")
    framed[...] = jnp.zeros_like(framed)
    framed[pl.ds(1, depth), pl.ds(1, rows)] = block[...]

    def there(dz, dy):
        inside = (gz + dz >= 0) & (gz + dz < n_gz) & (xy + dy >= 0) & (xy + dy < n_xy)
        return inside, (gz + dz, xy + dy)

    def span(step, size, far):
        if step == 0:
            return pl.ds(1, size) if far else pl.ds(0, size)
        if far:
            return pl.ds(0, 1) if step > 0 else pl.ds(size + 1, 1)
        return pl.ds(size - 1, 1) if step > 0 else pl.ds(0, 1)

    def copy(dz, dy, number):
        _, where = there(dz, dy)
        return pltpu.make_async_remote_copy(
            src_ref=block.at[span(dz, depth, False), span(dy, rows, False)],
            dst_ref=framed.at[span(dz, depth, True), span(dy, rows, True)],
            send_sem=send.at[number],
            recv_sem=recv.at[number],
            device_id=where,
            device_id_type=pl.DeviceIdType.MESH,
        )

    barrier = pltpu.get_barrier_semaphore()
    for dz, dy in neighbours():
        inside, where = there(dz, dy)

        @pl.when(inside)
        def _():
            pl.semaphore_signal(
                barrier, inc=1, device_id=where, device_id_type=pl.DeviceIdType.MESH
            )

    across = 1 + lax.min(gz, 1) + lax.min(n_gz - 1 - gz, 1)
    along = 1 + lax.min(xy, 1) + lax.min(n_xy - 1 - xy, 1)
    pl.semaphore_wait(barrier, across * along - 1)

    for number, (dz, dy) in enumerate(neighbours()):

        @pl.when(there(dz, dy)[0])
        def _():
            copy(dz, dy, number).start()

    for number, (dz, dy) in enumerate(neighbours()):

        @pl.when(there(dz, dy)[0])
        def _():
            copy(dz, dy, number).wait_send()

        @pl.when(there(-dz, -dy)[0])
        def _():
            copy(dz, dy, number).wait_recv()


def with_rims(block, collective_id, n_gz, n_xy):
    depth, rows, pairs, lanes = block.shape
    return pl.pallas_call(
        functools.partial(rim_kernel, n_gz, n_xy),
        out_shape=jax.ShapeDtypeStruct((depth + 2, rows + 2, pairs, lanes), block.dtype),
        in_specs=[VMEM],
        out_specs=VMEM,
        scratch_shapes=[pltpu.SemaphoreType.DMA((8,))] * 2,
        compiler_params=pltpu.CompilerParams(collective_id=collective_id, has_side_effects=True),
    )(block)


def weight_halves(weight, half, turned):
    lows, highs = [], []
    count = weight.shape[1] // half
    for first in range(0, count, 2):
        if first + 1 < count:
            near = weight[:, pl.ds(first * half, 2 * half)].astype(F32)
        else:
            last = weight[:, pl.ds(first * half, half)].astype(F32)
            near = jnp.concatenate([last, jnp.zeros_like(last)], axis=1)
        far = pltpu.roll(near, half, 1)
        if turned:
            both = jnp.concatenate([near, far], axis=0).T
            near, far = both[:half], both[half:]
        lows += [near, far]
        highs += [far, near]
    return lows, highs


def fill_band(target, weight, turned):
    half = weight.shape[0]
    lows, highs = weight_halves(weight, half, turned)
    low = lax.broadcasted_iota(jnp.int32, (half, 2 * half), 1) < half
    for offset in range(9):
        ks = [26 - 3 * offset - x if turned else 3 * offset + x for x in range(3)]
        parts = [
            jnp.where(low, lows[ks[1]], highs[ks[0]]),
            jnp.where(low, lows[ks[2]], highs[ks[1]]),
            jnp.where(low, 0.0, highs[ks[2]]),
            jnp.where(low, lows[ks[0]], 0.0),
        ]
        for place, part in enumerate(parts):
            target[pl.ds((4 * offset + place) * half, half), :] = part.astype(BF16)


def side_lanes(cells, half, period):
    pairs = cells.shape[1]
    lane = lax.broadcasted_iota(jnp.int32, cells.shape, 2)
    place = lax.broadcasted_iota(jnp.int32, cells.shape, 1) % period
    right = pltpu.roll(cells, pairs - 1, 1)
    left = pltpu.roll(cells, 1, 1)
    low = lane < half
    right = jnp.where(place == period - 1, 0.0, right)
    left = jnp.where(place == 0, 0.0, left)
    return jnp.where(low, right, left)


def fill_windows(target, source, half, period, inner):
    depth = target.shape[0]
    lanes = 2 * half
    if inner:
        target[...] = jnp.zeros_like(target)
    first, last = (1, depth - 1) if inner else (0, depth)
    for z in range(first, last):
        cells = source(z - first)
        rows = pl.ds(1, target.shape[1] - 2) if inner else pl.ds(0, target.shape[1])
        target[z, rows, :, pl.ds(0, lanes)] = cells.astype(BF16)
        target[z, rows, :, pl.ds(lanes, lanes)] = side_lanes(cells.astype(F32), half, period).astype(
            BF16
        )


def window_rows(windows, z, count, dz, dy):
    rows = windows.shape[1] - 2
    pairs, width = windows.shape[2], windows.shape[3]
    part = windows[pl.ds(z + dz, count), pl.ds(dy, rows)]
    return part.reshape(count * rows * pairs, width)


def conv_rows(windows, weight, z, count):
    parts = [window_rows(windows, z, count, dz, dy) for dz in range(3) for dy in range(3)]
    return jnp.dot(jnp.concatenate(parts, axis=1), weight[...], preferred_element_type=F32)


def outer_sums(out, base, windows, grad_turned, half):
    depth = windows.shape[0] - 2
    lanes = 2 * half
    lane = lax.broadcasted_iota(jnp.int32, (half, lanes), 1)
    held = None
    for offset in range(9):
        both = jnp.dot(
            grad_turned,
            window_rows(windows, 0, depth, offset // 3, offset % 3),
            preferred_element_type=F32,
        )
        top_near, top_far = both[:half, :lanes], both[:half, lanes:]
        far_turned = pltpu.roll(top_far, half, 1)
        near_turned = pltpu.roll(top_near, half, 1)
        first = jnp.where(lane < half, far_turned, near_turned) + both[half:, :lanes]
        third = near_turned + both[half:, lanes:]
        out[pl.ds(base + offset * half, half), :] = first.astype(BF16)
        if offset % 2 == 0:
            held = jnp.where(lane < half, third, 0.0)
        else:
            pair = held + jnp.where(lane < half, 0.0, pltpu.roll(third, half, 1))
            out[pl.ds(base + (9 + offset // 2) * half, half), :] = pair.astype(BF16)
    out[pl.ds(base + 13 * half, half), :] = held.astype(BF16)


def refine_kernel(
    period, vol, cot, back, refine, mix, fgrad, rsum, msum, xw, fw, pw, wb, wr, wrt, gate_s, pg_s
):
    depth, rows, pairs, lanes = fgrad.shape
    half = lanes // 2
    step = 4 if depth % 4 == 0 else depth
    flat = step * rows * pairs
    fill_band(wb, back, False)
    fill_band(wr, refine, False)
    fill_band(wrt, refine, True)
    mixed = mix[...].astype(F32)
    mixed = jnp.concatenate([mixed, jnp.zeros_like(mixed)], axis=1)
    mix2 = jnp.concatenate([mixed, pltpu.roll(mixed, half, 1)], axis=0).T.astype(BF16)
    fill_windows(xw, lambda z: vol[z], half, pairs, False)
    fw[...] = jnp.zeros_like(fw)
    pw[...] = jnp.zeros_like(pw)
    inner = pl.ds(1, rows)

    def put(target, z, cells):
        target[pl.ds(z + 1, step), inner, :, pl.ds(0, lanes)] = cells.astype(BF16)
        near = cells.astype(F32).reshape(step * rows, pairs, lanes)
        target[pl.ds(z + 1, step), inner, :, pl.ds(lanes, lanes)] = (
            side_lanes(near, half, period).astype(BF16).reshape(step, rows, pairs, lanes)
        )

    for z in range(0, depth, step):
        own = vol[pl.ds(z + 1, step), inner].astype(F32).reshape(flat, lanes)
        feature = (own + conv_rows(xw, wb, z, step)).astype(BF16)
        put(fw, z, feature.reshape(step, rows, pairs, lanes))
    for z in range(0, depth, step):
        pre = conv_rows(fw, wr, z, step)
        sig = jax.nn.sigmoid(pre)
        total = cot[pl.ds(z, step)].reshape(flat, lanes).astype(BF16)
        gate_s[pl.ds(z * rows * pairs, flat), :] = (pre * sig).astype(BF16)
        gated_grad = jnp.dot(total, mix2, preferred_element_type=F32)
        pre_grad = (gated_grad * sig * (1.0 + pre * (1.0 - sig))).astype(BF16)
        pg_s[pl.ds(z * rows * pairs, flat), :] = pre_grad
        put(pw, z, pre_grad.reshape(step, rows, pairs, lanes))
    for z in range(0, depth, step):
        total = cot[pl.ds(z, step)].reshape(flat, lanes)
        grad = total + conv_rows(pw, wrt, z, step)
        fgrad[pl.ds(z, step)] = grad.astype(BF16).reshape(step, rows, pairs, lanes)
    outer_sums(rsum, 0, fw, pg_s[...].T, half)
    cot_rows = cot[...].reshape(depth * rows * pairs, lanes).astype(BF16)
    both = jnp.dot(gate_s[...].T, cot_rows, preferred_element_type=F32)
    lane = lax.broadcasted_iota(jnp.int32, (half, lanes), 1)
    msum[...] = jnp.where(lane < half, both[:half] + pltpu.roll(both[half:], half, 1), 0.0).astype(
        BF16
    )


def backbone_kernel(vol, grad, back, rsum, msum, vgrad, sums, xw, gw, wbt):
    depth, rows, pairs, lanes = vgrad.shape
    half = lanes // 2
    step = 4 if depth % 4 == 0 else depth
    flat = step * rows * pairs
    fill_band(wbt, back, True)
    fill_windows(xw, lambda z: vol[z], half, pairs, False)
    fill_windows(gw, lambda z: grad[z], half, pairs, False)
    inner = pl.ds(1, rows)
    for z in range(0, depth, step):
        own = grad[pl.ds(z + 1, step), inner].astype(F32).reshape(flat, lanes)
        out = own + conv_rows(gw, wbt, z, step)
        vgrad[pl.ds(z, step)] = out.astype(BF16).reshape(step, rows, pairs, lanes)
    own = grad[pl.ds(1, depth), inner].reshape(depth * rows * pairs, lanes)
    outer_sums(sums, 0, xw, own.T, half)
    block = rsum.shape[0]
    sums[pl.ds(block, block), :] = rsum[...]
    sums[pl.ds(2 * block, half), :] = msum[...]
    used = 2 * block + half
    if used < sums.shape[0]:
        sums[pl.ds(used, sums.shape[0] - used), :] = jnp.zeros(
            (sums.shape[0] - used, lanes), BF16
        )


def total_kernel(n_gz, n_xy, sums, out, got1, part, got2, mine, *sems):
    gz, xy = lax.axis_index("gz"), lax.axis_index("xy")
    chunk = mine.shape[0]
    block = part.shape[0]
    barrier = pltpu.get_barrier_semaphore()

    def peer(axis, step):
        if axis == "gz":
            target = lax.rem(gz + step, n_gz)
            return target, (target, xy)
        target = lax.rem(xy + step, n_xy)
        return target, (gz, target)

    sizes = {"gz": n_gz, "xy": n_xy}

    def each(axis, action):
        def one(step, carry):
            action(step)
            return carry

        lax.fori_loop(1, sizes[axis], one, 0)

    def greet(axis):
        def one(step):
            pl.semaphore_signal(
                barrier,
                inc=1,
                device_id=peer(axis, step)[1],
                device_id_type=pl.DeviceIdType.MESH,
            )

        each(axis, one)

    greet("gz")
    greet("xy")
    pl.semaphore_wait(barrier, n_gz + n_xy - 2)

    def copy(axis, stage, source, target):
        def make(step):
            where, device = peer(axis, step)
            return pltpu.make_async_remote_copy(
                src_ref=source(where),
                dst_ref=target(step),
                send_sem=sems[2 * stage].at[step],
                recv_sem=sems[2 * stage + 1].at[step],
                device_id=device,
                device_id_type=pl.DeviceIdType.MESH,
            )

        return make

    blocks = copy("gz", 0, lambda w: sums.at[pl.ds(w * block, block)], lambda s: got1.at[s])
    each("gz", lambda step: blocks(step).start())
    each("gz", lambda step: blocks(step).wait_recv())
    total = sums[pl.ds(gz * block, block), :].astype(F32)
    for step in range(1, n_gz):
        total = total + got1[step].astype(F32)
    part[...] = total.astype(BF16)
    chunks = copy("xy", 1, lambda w: part.at[pl.ds(w * chunk, chunk)], lambda s: got2.at[s])
    each("xy", lambda step: chunks(step).start())
    each("xy", lambda step: chunks(step).wait_recv())
    total = part[pl.ds(xy * chunk, chunk), :].astype(F32)
    for step in range(1, n_xy):
        total = total + got2[step].astype(F32)
    mine[...] = total.astype(BF16)
    own = pl.ds(gz * block + xy * chunk, chunk)
    spread = copy("xy", 2, lambda w: mine, lambda s: out.at[own])
    each("xy", lambda step: spread(step).start())
    out[own, :] = mine[...]
    each("xy", lambda step: spread(step).wait_recv())
    ours = pl.ds(gz * block, block)
    again = copy("gz", 3, lambda w: out.at[ours], lambda s: out.at[ours])
    each("gz", lambda step: again(step).start())
    each("gz", lambda step: blocks(step).wait_send())
    each("xy", lambda step: chunks(step).wait_send())
    each("xy", lambda step: spread(step).wait_send())
    each("gz", lambda step: again(step).wait())


def finish_kernel(totals, back_step, refine_step, mix_step):
    half = mix_step.shape[0]
    lanes = 2 * half
    block = 14 * half
    low = lax.broadcasted_iota(jnp.int32, (half, lanes), 1) < half

    def scale_of(values, count):
        squares = jnp.sum(values * values, axis=0, keepdims=True)
        return jnp.sqrt(jnp.sum(squares, axis=1, keepdims=True) / count + EPSILON)

    for base, out in ((0, back_step), (block, refine_step)):
        values = totals[pl.ds(base, block), :].astype(F32)
        scale = scale_of(values, 27.0 * half * half)
        lows, highs = [None] * 28, [None] * 28
        for tile in range(14):
            near = values[tile * half : (tile + 1) * half]
            both = jnp.concatenate([near, pltpu.roll(near, half, 1)], axis=0).T / scale
            if tile < 9:
                first, second = 3 * tile, 3 * tile + 1
            else:
                first, second = 6 * (tile - 9) + 2, 6 * (tile - 9) + 5
            lows[first], highs[first] = both[:half], both[half:]
            if second < 27:
                lows[second], highs[second] = both[half:], both[:half]
        for k in range(0, 26, 2):
            out[:, pl.ds(k * half, lanes)] = jnp.where(low, lows[k], highs[k + 1])
        out[:, pl.ds(26 * half, half)] = lows[26][:, :half]
    values = totals[pl.ds(2 * block, half), :].astype(F32)
    mix_step[...] = (values / scale_of(values, 1.0 * half * half))[:, :half]


def body(volume, backbone_weight, refine_weight, mix_weight, tile_cot, tile_slot, tile_count):
    depth, rows, width = volume.shape
    channels = mix_weight.shape[0]
    edge = tile_cot.shape[4]
    owners, capacity = tile_cot.shape[2], tile_cot.shape[3]
    assert depth == edge and rows == edge
    lanes = 2 * channels
    pairs = width // lanes
    period = edge // 2
    tiles = pairs // period
    slots = owners * capacity
    n_gz, n_xy = lax.axis_size("gz"), lax.axis_size("xy")
    devices = n_gz * n_xy
    brick = (depth, rows, pairs, lanes)
    rimmed = with_rims(volume.reshape(brick), 1, n_gz, n_xy)

    my_counts = jnp.sum(
        tile_count[0]
        * (jnp.arange(owners, dtype=jnp.int32) == lax.axis_index("xy")).astype(jnp.int32)[:, None],
        axis=0,
    )
    live = (jnp.arange(capacity, dtype=jnp.int32)[None, :] < my_counts[:, None]).reshape(slots)
    picker = (
        (tile_slot.reshape(slots)[None, :] == jnp.arange(tiles, dtype=jnp.int32)[:, None])
        & live[None, :]
    ).astype(BF16)
    cot = jnp.dot(
        picker, tile_cot.reshape(slots, edge * edge * edge * channels), preferred_element_type=F32
    )
    cot = cot.reshape(tiles, depth, rows, period, lanes).transpose(1, 2, 0, 3, 4).reshape(brick)

    block = 14 * channels
    framed = (depth + 2, rows + 2, pairs, 2 * lanes)
    params = pltpu.CompilerParams(vmem_limit_bytes=56 * 1024 * 1024)
    fgrad, rsum, msum = pl.pallas_call(
        functools.partial(refine_kernel, period),
        out_shape=(
            jax.ShapeDtypeStruct(brick, BF16),
            jax.ShapeDtypeStruct((block, lanes), BF16),
            jax.ShapeDtypeStruct((channels, lanes), BF16),
        ),
        in_specs=[VMEM] * 5,
        out_specs=(VMEM,) * 3,
        scratch_shapes=[
            pltpu.VMEM(framed, BF16),
            pltpu.VMEM(framed, BF16),
            pltpu.VMEM(framed, BF16),
            pltpu.VMEM((36 * channels, lanes), BF16),
            pltpu.VMEM((36 * channels, lanes), BF16),
            pltpu.VMEM((36 * channels, lanes), BF16),
            pltpu.VMEM((depth * rows * pairs, lanes), BF16),
            pltpu.VMEM((depth * rows * pairs, lanes), BF16),
        ],
        compiler_params=params,
    )(
        rimmed,
        cot,
        backbone_weight,
        refine_weight,
        mix_weight,
    )
    grad_rimmed = with_rims(fgrad, 2, n_gz, n_xy)
    used = 2 * block + channels
    chunk = -(-used // (devices * 16)) * 16
    vgrad, sums = pl.pallas_call(
        backbone_kernel,
        out_shape=(
            jax.ShapeDtypeStruct(brick, BF16),
            jax.ShapeDtypeStruct((devices * chunk, lanes), BF16),
        ),
        in_specs=[VMEM] * 5,
        out_specs=(VMEM,) * 2,
        scratch_shapes=[
            pltpu.VMEM(framed, BF16),
            pltpu.VMEM(framed, BF16),
            pltpu.VMEM((36 * channels, lanes), BF16),
        ],
        compiler_params=params,
    )(rimmed, grad_rimmed, backbone_weight, rsum, msum)
    totals = pl.pallas_call(
        functools.partial(total_kernel, n_gz, n_xy),
        out_shape=jax.ShapeDtypeStruct((devices * chunk, lanes), BF16),
        in_specs=[VMEM],
        out_specs=VMEM,
        scratch_shapes=[
            pltpu.VMEM((n_gz, n_xy * chunk, lanes), BF16),
            pltpu.VMEM((n_xy * chunk, lanes), BF16),
            pltpu.VMEM((n_xy, chunk, lanes), BF16),
            pltpu.VMEM((chunk, lanes), BF16),
        ]
        + [pltpu.SemaphoreType.DMA((n,)) for n in (n_gz, n_gz, n_xy, n_xy, n_xy, n_xy, n_gz, n_gz)],
        compiler_params=pltpu.CompilerParams(collective_id=0, has_side_effects=True),
    )(sums)
    wide = jax.ShapeDtypeStruct((channels, 27 * channels), F32)
    back_step, refine_step, mix_step = pl.pallas_call(
        finish_kernel,
        out_shape=(wide, wide, jax.ShapeDtypeStruct((channels, channels), F32)),
        in_specs=[VMEM],
        out_specs=(VMEM,) * 3,
    )(totals)
    return (vgrad.reshape(depth, rows, width), back_step, refine_step, mix_step)


def solution(mesh):
    in_specs = (
        P("gz", "xy", None),
        P(),
        P(),
        P(),
        P("gz", "xy", None, None, None, None, None),
        P("gz", "xy", None, None),
        P("gz", None, None),
    )
    out_specs = (P("gz", "xy", None), P(), P(), P())
    return jax.shard_map(body, mesh=mesh, in_specs=in_specs, out_specs=out_specs, check_vma=False)
```
